32 devices in a mesh: groups: 2 (over x), row: 16 (over z, y, core).
Axes of the slice: x: 2, y: 2, z: 4, core: 2. Of those that a mesh axis runs over, the one named last changes fastest.
Arguments:
- design_rows: bfloat16 [1536, 2048], P('groups', 'row'), parts along dimension 0, may hold values from -6 to 6
- design_cols: bfloat16 [1536, 2048], P('groups', 'row'), parts along dimension 0, may hold values from -0.21875 to 0.21875
- noise_std: float32 [1536], P('groups'), parts along dimension 0, may hold values from 0.3 to 1
- record_noise_amplitude: float32 [32], P(('groups', 'row')), parts along dimension 0, may hold values from 0.5 to 2
- record_correlation_length: float32 [32], P(('groups', 'row')), parts along dimension 0, may hold values from 2 to 32
- arc_lengths: int32 [24], P('groups'), parts along dimension 0, may hold values from 1 to 128, 768 in all
- arc_record_index: int32 [24], P('groups'), parts along dimension 0, may hold values from 0 to 15
- block_map: int32 [32], P('groups'), parts along dimension 0, may hold values from 0 to 15, each once
Outputs:
- normal_block: float32 [4096, 2048], P(('groups', 'row')), parts along dimension 0
The draws below stay inside these ranges and needn't reach their ends.
There are 2 independent parts, one for each index of `groups`. The reference program is written for one: setup_inputs(seed, part) draws one part's arguments, and reference() takes and returns one part's arrays. A program takes and returns all parts, laid end to end along the dimension named above; each array names one. Nothing has to cross between parts.
Inputs may be any that keep to these rules, and one draw needn't show every extreme that they name: `arc_lengths`: arcs are whole runs of observations laid end to end from the first; the lengths sum to 768 and the longest has exactly 128. `block_map`: each column block number once.
All inputs are finite; a program needn't handle non-finite values.
Results may differ from the reference program's by a relative error of at most 0.0037.
Values may be sent and summed in bfloat16 or wider, within the bound.
No kernel may reach another device: no remote copies, remote signals or barrier semaphores. Data moves between devices by JAX's collectives and lax.ppermute only.
A program may use at most 128 MiB of HBM per device.

```python
import math
import jax
import jax.numpy as jnp
import numpy as np
from jax import lax

OBS = 768
ARC_TOTAL = 12
AM = 128
CB = 128
NR = 2048
NB = 16
NC = 2048
RECORD_TOTAL = 16


def place_ends(drawn, rng, smallest, high):
    index_at = [jax.random.randint(jax.random.fold_in(rng, axis), (), 0, length) for axis, length in enumerate(drawn.shape)]
    main_axis = drawn.shape.index(max(drawn.shape))
    next_to = index_at[:main_axis] + [(index_at[main_axis] + 1) % drawn.shape[main_axis]] + index_at[main_axis + 1:]
    return drawn.at[tuple(index_at)].set(smallest).at[tuple(next_to)].set(high)


def level_of(own_key, shape, cuts, low, high):
    gain = 1.0
    for axis_at, parts in cuts:
        draws = jax.random.uniform(jax.random.fold_in(jax.random.fold_in(own_key, 6), axis_at), (parts,), jnp.float32, low / len(cuts), high / len(cuts))
        gain = gain * jnp.repeat(jnp.exp(draws), shape[axis_at] // parts).reshape((-1,) + (1,) * (len(shape) - 1 - axis_at))
    return gain


def length_profile(count, total, most, skew):
    portions = [(1 << 20) // math.isqrt(standing ** skew) + 1 for standing in range(2, count + 1)]
    rest, holding = total - most - (count - 1), [1] * (count - 1)
    while rest > 0:
        free = [i for i in range(count - 1) if holding[i] < most]
        whole, budget = sum([portions[i] for i in free]), rest
        for i in free:
            addition = min(most - holding[i], max(1, budget * portions[i] // whole), rest)
            holding[i] = holding[i] + addition
            rest = rest - addition
    return np.array([most] + holding)


def uneven_parts(key, number_of, total, bound, slope):
    if number_of == 2:
        one = jax.random.randint(key, (), max(1, total - bound), min(bound, total - 1) + 1)
        return jnp.stack([one, total - one])
    sizes = jnp.asarray(length_profile(number_of, total, bound, slope), jnp.int32)
    couples = (number_of - 1) // 2
    source_of, receiver = sizes[1:1 + 2 * couples:2], sizes[2:2 + 2 * couples:2]
    slack = jnp.minimum(source_of - 1, bound - receiver)
    moved = jax.random.randint(jax.random.fold_in(key, 1), (couples,), 0, 1 << 20) % (slack + 1)
    sizes = sizes.at[1:1 + 2 * couples:2].set(source_of - moved).at[2:2 + 2 * couples:2].set(receiver + moved)
    return sizes[jax.random.permutation(jax.random.fold_in(key, 2), number_of)]


def scatter_about(rng, dims, width, limit, split=(), held_as=jnp.bfloat16):
    result = jax.random.normal(rng, dims, jnp.float32) * width
    if len(split) > 0:
        result = level_of(rng, dims, split, -0.22, 0.18) * result
    return jnp.clip(result, min=-limit, max=limit).astype(held_as)


def setup_inputs(seed: int = 0, part: int = 0) -> dict:
    seeds = jax.random.split(jax.random.key(seed), 9)
    part_keys = jax.random.split(jax.random.fold_in(seeds[8], part), 9)
    return {
        "design_rows": scatter_about(part_keys[0], (OBS, NR), 1.0, 6.0, ((1, 16),)),
        "design_cols": scatter_about(part_keys[1], (OBS, NC), OBS ** -0.5, 0.21875, ((1, 16),)),
        "noise_std": jnp.clip(jnp.exp(jax.random.uniform(part_keys[2], (OBS,), jnp.float32, math.log(0.3), math.log(1.0))), 0.3, 1.0),
        "record_noise_amplitude": jnp.clip(jnp.exp(math.log(2.0) - 1.3862944 * jax.random.uniform(part_keys[3], (RECORD_TOTAL,), jnp.float32) ** level_of(part_keys[3], (RECORD_TOTAL,), ((0, 16),), -0.2, 0.2)), 0.5, 2.0),
        "record_correlation_length": jnp.clip(jnp.exp(math.log(32.0) - 2.7725887 * jax.random.uniform(part_keys[4], (RECORD_TOTAL,), jnp.float32) ** level_of(part_keys[4], (RECORD_TOTAL,), ((0, 16),), -0.2, 0.2)), 2.0, 32.0),
        "arc_lengths": uneven_parts(part_keys[5], ARC_TOTAL, OBS, AM, 2).astype(jnp.int32),
        "arc_record_index": place_ends(jax.random.randint(part_keys[6], (ARC_TOTAL,), 0, RECORD_TOTAL), jax.random.fold_in(part_keys[6], 1), 0, RECORD_TOTAL - 1).astype(jnp.int32),
        "block_map": jax.random.permutation(part_keys[7], NB).astype(jnp.int32),
    }


def arc_starts(arc_lengths):
    endings = jnp.cumsum(arc_lengths).astype(jnp.int32)
    return (endings - arc_lengths).astype(jnp.int32)

def whitening(starts, arc_lengths, amplitudes, correlation, noise_std):
    offsets = jnp.arange(AM, dtype=jnp.int32)
    inside = offsets[None, :] < arc_lengths[:, None]
    indices = jnp.minimum(starts[:, None] + offsets[None, :], OBS - 1).astype(jnp.int32)
    noise_level = noise_std[indices]
    observation_separation = jnp.abs(offsets[:, None] - offsets[None, :]).astype(jnp.float32)
    kernel = (amplitudes * amplitudes)[:, None, None] * jnp.exp(-observation_separation[None, :, :] / correlation[:, None, None])
    live_pair = inside[:, :, None] & inside[:, None, :]
    identity = jnp.eye(AM, dtype=jnp.float32)
    covariance = jnp.where(live_pair, kernel + identity[None, :, :] * (noise_level * noise_level)[:, :, None], identity[None, :, :])
    cholesky_factor = jnp.linalg.cholesky(covariance)
    return lax.linalg.triangular_solve(cholesky_factor, jnp.broadcast_to(identity, cholesky_factor.shape), left_side=True, lower=True)

def whiten(design, starts, arc_lengths, inverse):
    offsets = jnp.arange(AM, dtype=jnp.int32)
    inside = offsets[None, :] < arc_lengths[:, None]
    indices = jnp.minimum(starts[:, None] + offsets[None, :], OBS - 1).astype(jnp.int32)
    padded = jnp.where(inside[:, :, None], design[indices].astype(jnp.float32), jnp.float32(0.0))
    mixed = jnp.einsum('kab,kbn->kan', inverse, padded, precision=lax.Precision.HIGHEST)
    observed = jnp.arange(OBS, dtype=jnp.int32)
    arc_index = jnp.sum((starts[:, None] <= observed[None, :]).astype(jnp.int32), axis=0) - 1
    arc_place = observed - starts[arc_index]
    stacked = mixed.reshape(ARC_TOTAL * AM, design.shape[1])
    return stacked[arc_index * AM + arc_place].astype(jnp.bfloat16)

def reference(design_rows, design_cols, noise_std, record_noise_amplitude, record_correlation_length, arc_lengths, arc_record_index, block_map):
    starts = arc_starts(arc_lengths)
    inverse = whitening(starts, arc_lengths, record_noise_amplitude[arc_record_index], record_correlation_length[arc_record_index], noise_std)
    rows_white = whiten(design_rows, starts, arc_lengths, inverse)
    cols_white = whiten(design_cols, starts, arc_lengths, inverse)
    blocks = cols_white.reshape(OBS, NB, CB)[:, block_map, :].reshape(OBS, NC)
    return lax.dot_general(rows_white.astype(jnp.float32), blocks.astype(jnp.float32), (((0,), (0,)), ((), ())), preferred_element_type=jnp.float32)
```

```python
import functools

import jax
import jax.numpy as jnp
from jax import lax
from jax.experimental import pallas as pl
from jax.experimental.pallas import tpu as pltpu
from jax.sharding import PartitionSpec as P

AM = 128
LANES = 128


def shifts():
    s, out = 1, []
    while s < AM:
        out.append(s)
        s *= 2
    return out


def prep_kernel(par, lens, rec, noise_ref, rows_ref, z_ref, data, fwd, bwd, lane):
    obs, width = rows_ref.shape
    me = lax.axis_index("row")
    place = lax.broadcasted_iota(jnp.int32, (8, obs), 1)
    start = jnp.int32(0)
    first = place < 0
    amp = jnp.zeros((8, obs), jnp.float32)
    length = jnp.ones((8, obs), jnp.float32)
    for k in range(lens.shape[0]):
        slot = lax.bitwise_xor(me, rec[k])
        here = place >= start
        amp = jnp.where(here, par[2 * slot], amp)
        length = jnp.where(here, par[2 * slot + 1], length)
        first = jnp.logical_or(first, place == start)
        start = start + lens[k]
    back = functools.partial(pltpu.roll, axis=1)
    ahead = lambda x, s: pltpu.roll(x, obs - s, axis=1)
    noise = jnp.broadcast_to(noise_ref[...], (8, obs))
    sig2 = noise * noise
    a2 = amp * amp
    phi = jnp.exp(-1.0 / length)
    q = a2 * (1.0 - phi * phi)
    prev = back(sig2, 1)
    ma = jnp.where(first, 0.0, phi * phi * prev + q)
    mb = jnp.where(first, a2, q * prev)
    mc = jnp.where(first, 0.0, 1.0)
    md = jnp.where(first, 1.0, prev)
    for s in shifts():
        ra, rb, rc, rd = back(ma, s), back(mb, s), back(mc, s), back(md, s)
        na, nb = ma * ra + mb * rc, ma * rb + mb * rd
        nc, nd = mc * ra + md * rc, mc * rb + md * rd
        norm = 1.0 / (nc + nd)
        ma, mb, mc, md = na * norm, nb * norm, nc * norm, nd * norm
    pred = (ma + mb) / (mc + md)
    inv = 1.0 / (pred + sig2)
    gain = pred * inv
    alpha = phi * sig2 * inv
    keep = jnp.where(first, 0.0, 1.0)
    keep_next = ahead(keep, 1)
    lane[0] = phi * gain
    lane[1] = keep
    lane[2] = inv
    lane[3] = phi
    lane[4] = keep_next
    lane[5] = gain
    af = keep * back(alpha, 1)
    ab = keep_next * ahead(alpha, 1)
    for l, s in enumerate(shifts()):
        fwd[l] = af
        bwd[l] = ab
        af = af * back(af, s)
        ab = ab * ahead(ab, s)
    data[...] = rows_ref[...].astype(jnp.float32).T

    def two(x):
        return jnp.concatenate([x, x], axis=0)

    def chunk(i, carry):
        at = pl.ds(pl.multiple_of(i * 16, 16), 16)
        y = data[at, :]
        b = two(lane[1]) * back(two(lane[0]) * y, 1)
        for l, s in enumerate(shifts()):
            b = b + two(fwd[l]) * back(b, s)
        w = (y - b) * two(lane[2])
        b = two(lane[4]) * ahead(two(lane[3]) * w, 1)
        for l, s in enumerate(shifts()):
            b = b + two(bwd[l]) * ahead(b, s)
        z = w - two(lane[5]) * b
        hi = z.astype(jnp.bfloat16)
        z_ref[at, :] = hi
        z_ref[pl.ds(pl.multiple_of(i * 16 + width, 16), 16), :] = (
            z - hi.astype(jnp.float32)
        ).astype(jnp.bfloat16)
        return carry

    lax.fori_loop(0, width // 16, chunk, 0)


def prepare(params, lens, rec, noise, rows):
    obs, width = rows.shape
    levels = len(shifts())
    smem = pl.BlockSpec(memory_space=pltpu.SMEM)
    vmem = pl.BlockSpec(memory_space=pltpu.VMEM)
    return pl.pallas_call(
        prep_kernel,
        name="prepare",
        out_shape=jax.ShapeDtypeStruct((2 * width, obs), jnp.bfloat16),
        in_specs=[smem, smem, smem, vmem, vmem],
        out_specs=vmem,
        scratch_shapes=[
            pltpu.VMEM((width, obs), jnp.float32),
            pltpu.VMEM((levels, 8, obs), jnp.float32),
            pltpu.VMEM((levels, 8, obs), jnp.float32),
            pltpu.VMEM((6, 8, obs), jnp.float32),
        ],
        cost_estimate=pl.CostEstimate(flops=2000000, bytes_accessed=3000000, transcendentals=0),
    )(params, lens, rec, noise.reshape(1, obs), rows)


def product_kernel(slots, aliased, block_map, z_ref, *refs):
    n = len(slots)
    blocks, refs = refs[:n], refs[n + (1 if aliased else 0) :]
    out, held, made, sem_in, sem_out = refs
    me = lax.axis_index("row")
    width = z_ref.shape[0] // 2
    copies = [pltpu.make_async_copy(blocks[i], held.at[i], sem_in.at[i]) for i in range(n)]
    for c in copies:
        c.start()

    def position(slot):
        want = lax.bitwise_xor(me, slot)

        def look(p, found):
            return jnp.where(block_map[p] == want, p, found)

        return lax.fori_loop(0, block_map.shape[0], look, jnp.int32(0))

    stores = []
    for i in range(0, n, 2):
        group = range(i, min(i + 2, n))
        for j in group:
            copies[j].wait()
        cols = jnp.concatenate([held[j] for j in group], axis=1)
        r = lax.dot_general(z_ref[...], cols, (((1,), (0,)), ((), ())), preferred_element_type=jnp.float32)
        r = r[:width] + r[width:]
        for j in group:
            block = held.shape[2]
            made[j] = r[:, (j - i) * block : (j - i + 1) * block]
            at = pl.ds(pl.multiple_of(position(slots[j]) * block, block), block)
            s = pltpu.make_async_copy(made.at[j], out.at[:, at], sem_out.at[j])
            s.start()
            stores.append(s)
    for s in stores:
        s.wait()


def product(z, block_map, blocks, slots, total, into):
    obs, block = blocks[0].shape
    width = z.shape[0] // 2
    n = len(blocks)
    anyspace = pl.BlockSpec(memory_space=pl.ANY)
    aliased = into is not None
    extra = [into] if aliased else []
    return pl.pallas_call(
        functools.partial(product_kernel, tuple(slots), aliased),
        name="product",
        out_shape=jax.ShapeDtypeStruct((width, total), jnp.float32),
        in_specs=[pl.BlockSpec(memory_space=pltpu.SMEM), pl.BlockSpec(memory_space=pltpu.VMEM)]
        + [anyspace] * (n + len(extra)),
        out_specs=anyspace,
        scratch_shapes=[
            pltpu.VMEM((n, obs, block), jnp.bfloat16),
            pltpu.VMEM((n, width, block), jnp.float32),
            pltpu.SemaphoreType.DMA((n,)),
            pltpu.SemaphoreType.DMA((n,)),
        ],
        input_output_aliases={2 + n: 0} if aliased else {},
        cost_estimate=pl.CostEstimate(
            flops=4 * n * width * block * obs, bytes_accessed=n * (obs * block * 2 + width * block * 4), transcendentals=0
        ),
    )(block_map, z, *blocks, *extra)


def per_device(dims, rows, cols, noise, amplitude, correlation, lens, rec, block_map):
    na, nb, nc = dims
    size = na * nb * nc

    def swap(x, mask):
        return lax.ppermute(x, "row", [(i, i ^ mask) for i in range(size)])

    params = jnp.concatenate([amplitude, correlation])
    step = 1
    while step < nc * nb:
        params = jnp.concatenate([params, swap(params, step)])
        step *= 2
    params = jnp.concatenate([params] + [swap(params, k * nb * nc) for k in range(1, na)])

    held = {0: cols}
    for k in range(1, na):
        held[k * nb * nc] = swap(cols, k * nb * nc)
    for slot in list(held):
        for k in range(1, nb):
            held[slot + k * nc] = swap(held[slot], k * nc)
    for slot in list(held):
        for k in range(1, nc):
            held[slot + k] = swap(held[slot], k)

    z = prepare(params, lens, rec, noise, rows)
    total = cols.shape[1] * size
    late = [s for s in held if s // (nb * nc) >= na // 2 and (s // nc) % nb != 0]
    early = [s for s in held if s not in late]
    early.sort(key=lambda s: (s // nc, s % nc))
    late.sort(key=lambda s: (s // nc, s % nc))
    out = product(z, block_map, [held[s] for s in early], early, total, None)
    return product(z, block_map, [held[s] for s in late], late, total, out)


def row_dims(mesh):
    size = mesh.shape["row"]
    half = size // 2
    nb = 1
    while (nb * 2) ** 2 <= half:
        nb *= 2
    return half // nb, nb, 2


def solution(mesh):
    return jax.shard_map(
        functools.partial(per_device, row_dims(mesh)),
        mesh=mesh,
        in_specs=(
            P("groups", "row"),
            P("groups", "row"),
            P("groups"),
            P(("groups", "row")),
            P(("groups", "row")),
            P("groups"),
            P("groups"),
            P("groups"),
        ),
        out_specs=P(("groups", "row"), None),
        check_vma=False,
    )
```
